32 devices in a mesh: row: 4 (over z), col: 8 (over y, x, core).
Axes of the slice: x: 2, y: 2, z: 4, core: 2. Of those that a mesh axis runs over, the one named last changes fastest.
Arguments:
- inv_depth: float32 [64, 3072], P(('row', 'col')), may hold values from 0.2 to 1
- rotation: float32 [3, 64], P(None, ('row', 'col')), may hold values from -0.05 to 0.05
- translation: float32 [3, 64], P(None, ('row', 'col')), may hold values from -0.25 to 0.25
- edge_target: int32 [64, 24], P(('row', 'col')), may hold values from 0 to 63, as said below
- flow_obs: float32 [2, 64, 24, 3072], P(None, ('row', 'col')), may hold values from -2.8 to 2.8
- weight: float32 [2, 64, 24, 3072], P(None, ('row', 'col')), may hold values from 0.1 to 1
Outputs:
- depth_next: float32 [64, 3072], P(('row', 'col'))
- pose_step: float32 [6, 64], P(None, ('row', 'col'))
The draws below stay inside these ranges and needn't reach their ends.
Inputs may be any that keep to these rules, and one draw needn't show every extreme that they name: `edge_target`: each keyframe's targets are distinct, differ from the keyframe itself, are sorted ascending, and lie in the keyframe's own block of 16 consecutive keyframes or in one of the two neighbouring blocks, the blocks counted cyclically.
All inputs are finite; a program needn't handle non-finite values.
Results may differ from the reference program's by a relative error of at most 0.0003.
Values sent between devices are 32-bit elements; how exact they have to be, the bound alone decides.
No kernel may reach another device: no remote copies, remote signals or barrier semaphores. Data moves between devices by JAX's collectives and lax.ppermute only.
A program may use at most 128 MiB of HBM per device.

```python
import math
import jax
import jax.numpy as jnp
from jax import lax

IMG_H = 48
IMG_W = 64
PIXELS = 3072
F_DEV = 2
E_FRAME = 24
GROUP = 16
FRAMES = 64


def draw_edge_target(key, part):
    base_key = jax.random.fold_in(key, 11)
    key_pop, key_mix = jax.random.split(base_key)
    frames = jnp.arange(FRAMES, dtype=jnp.int32)
    group_id = frames // GROUP
    candidates = 3 * GROUP
    popular = jax.random.randint(key_pop, (FRAMES,), 0, 4) * 16384
    jitter = jax.random.randint(key_mix, (FRAMES, candidates), 0, 65536)
    cand_index = jnp.arange(candidates, dtype=jnp.int32)
    cand_group = (group_id[:, None] - 1 + cand_index[None, :] // GROUP + FRAMES // GROUP) % (FRAMES // GROUP)
    cand_frame = cand_group * GROUP + cand_index[None, :] % GROUP
    scores = jitter + jnp.take(popular, cand_frame)
    scores = jnp.where(cand_frame == frames[:, None], -1, scores)
    scores = scores * 4096 + cand_index[None, :]
    _, picked = lax.top_k(scores, E_FRAME)
    chosen = jnp.take_along_axis(cand_frame, picked, 1)
    return jnp.sort(chosen, 1).astype(jnp.int32)


def draw_flow_obs(key, part):
    base_key = jax.random.fold_in(key, 23)
    key_bias, key_noise = jax.random.split(base_key)
    offset_part = 0.4 * jnp.clip(jax.random.normal(key_bias, (2, FRAMES, E_FRAME, 1), jnp.float32), -4.0, 4.0)
    jitter = 0.3 * jnp.clip(jax.random.normal(key_noise, (2, FRAMES, E_FRAME, PIXELS), jnp.float32), -4.0, 4.0)
    return (offset_part + jitter).astype(jnp.float32)


def block_levels(own_key, extent, cuts, smallest, high):
    loudness, own = 1.0, jax.random.fold_in(own_key, 6)
    for axis_at, parts in cuts:
        steps = jnp.exp(jax.random.uniform(jax.random.fold_in(own, axis_at), (parts,), jnp.float32, smallest / len(cuts), high / len(cuts)))
        loudness = loudness * jnp.repeat(steps, extent[axis_at] // parts).reshape([-1 if axis == axis_at else 1 for axis in range(len(extent))])
    return loudness


def setup_inputs(seed: int = 0) -> dict:
    key_of = jax.random.split(jax.random.key(seed), 7)
    inv_depth = jnp.clip(jnp.exp(math.log(1.0) - 1.609438 * jax.random.uniform(key_of[0], (FRAMES, PIXELS), jnp.float32) ** block_levels(key_of[0], (FRAMES, PIXELS), ((0, 32),), -0.2, 0.2)), 0.2, 1.0)
    rotation = jnp.clip(jax.random.uniform(key_of[1], (3, FRAMES), jnp.float32, -0.05, 0.05) * block_levels(key_of[1], (3, FRAMES), ((1, 32),), -0.4, 0.0), -0.05, 0.05)
    translation = jnp.clip(jax.random.uniform(key_of[2], (3, FRAMES), jnp.float32, -0.25, 0.25) * block_levels(key_of[2], (3, FRAMES), ((1, 32),), -0.4, 0.0), -0.25, 0.25)
    edge_target = draw_edge_target(jax.random.fold_in(key_of[6], 71), 0)
    flow_obs = draw_flow_obs(jax.random.fold_in(key_of[6], 71), 0)
    weight = jnp.clip(jnp.exp(math.log(1.0) - 2.3025851 * jax.random.uniform(key_of[5], (2, FRAMES, E_FRAME, PIXELS), jnp.float32) ** block_levels(key_of[5], (2, FRAMES, E_FRAME, PIXELS), ((1, 32),), -0.2, 0.2)), 0.1, 1.0)
    return {"inv_depth": inv_depth, "rotation": rotation, "translation": translation, "edge_target": edge_target, "flow_obs": flow_obs, "weight": weight}


PRECISE = lax.Precision.HIGHEST
DAMP_DEPTH = 0.1
LEVENBERG = 0.1
RIDGE = 0.001

def pixel_grid(pixel_count):
    pixel_index = jnp.arange(pixel_count, dtype=jnp.int32)
    across = (pixel_index % IMG_W).astype(jnp.float32)
    downward = (pixel_index // IMG_W).astype(jnp.float32)
    return ((across + 0.5) / IMG_W - 0.5, (downward + 0.5 - 0.5 * IMG_H) / IMG_W)

def edge_terms(relative, target_depth, flows, weights, across, downward):
    spin_x, spin_y, spin_z, move_x, move_y, move_z = [relative[i][:, None] for i in range(6)]
    point_x = across + spin_y - spin_z * downward + move_x * target_depth
    point_y = downward + spin_z * across - spin_x + move_y * target_depth
    point_z = 1.0 + spin_x * downward - spin_y * across + move_z * target_depth
    recip_z = 1.0 / point_z
    image_u = point_x * recip_z
    image_v = point_y * recip_z
    resid_u = flows[0] - (image_u - across)
    resid_v = flows[1] - (image_v - downward)
    slope_u = recip_z * (move_x - image_u * move_z)
    slope_v = recip_z * (move_y - image_v * move_z)
    depth_recip = target_depth * recip_z
    blank_map = jnp.zeros_like(recip_z)
    jac_u = jnp.stack([-image_u * downward * recip_z, (1.0 + image_u * across) * recip_z, -downward * recip_z, depth_recip, blank_map, -image_u * depth_recip])
    jac_v = jnp.stack([(-1.0 - image_v * downward) * recip_z, image_v * across * recip_z, across * recip_z, blank_map, depth_recip, -image_v * depth_recip])
    weight_u = weights[0]
    weight_v = weights[1]
    depth_grad = weight_u * slope_u * resid_u + weight_v * slope_v * resid_v
    depth_curv = weight_u * slope_u * slope_u + weight_v * slope_v * slope_v
    scaled_u = weight_u * jac_u
    scaled_v = weight_v * jac_v
    coupling = scaled_u * slope_u + scaled_v * slope_v
    block = jnp.einsum('aep,bep->eab', scaled_u, jac_u, precision=PRECISE) + jnp.einsum('aep,bep->eab', scaled_v, jac_v, precision=PRECISE)
    pose_grad = jnp.einsum('aep,ep->ea', scaled_u, resid_u, precision=PRECISE) + jnp.einsum('aep,ep->ea', scaled_v, resid_v, precision=PRECISE)
    return (depth_grad, depth_curv, coupling, block, pose_grad)

def solve_frames(block_table):
    frame_count = block_table.shape[0]
    matrix = block_table[:, :36].reshape(frame_count, 6, 6).transpose(1, 2, 0)
    right_side = block_table[:, 36:].T
    factor = {}
    for i in range(6):
        for j in range(i + 1):
            element = matrix[i, j]
            if i == j:
                element = element * (1.0 + LEVENBERG) + RIDGE
            for k in range(j):
                element = element - factor[i, k] * factor[j, k]
            factor[i, j] = jnp.sqrt(element) if i == j else element / factor[j, j]
    forward = []
    for i in range(6):
        element = right_side[i]
        for k in range(i):
            element = element - factor[i, k] * forward[k]
        forward.append(element / factor[i, i])
    result = [None] * 6
    for i in reversed(range(6)):
        element = forward[i]
        for k in range(i + 1, 6):
            element = element - factor[k, i] * result[k]
        result[i] = element / factor[i, i]
    return jnp.stack(result, 1)

def reference(inv_depth, rotation, translation, edge_target, flow_obs, weight):
    across, downward = pixel_grid(PIXELS)
    blocks = FRAMES // F_DEV
    block_edges = F_DEV * E_FRAME
    targets = edge_target.reshape(blocks, block_edges)
    sources = (jnp.arange(FRAMES * E_FRAME, dtype=jnp.int32) // E_FRAME).reshape(blocks, block_edges)
    flows = flow_obs.reshape(2, blocks, block_edges, PIXELS).transpose(1, 0, 2, 3)
    weights = weight.reshape(2, blocks, block_edges, PIXELS).transpose(1, 0, 2, 3)
    pose_all = jnp.concatenate([rotation, translation], 0)
    pieces_all = (sources, targets, flows, weights)

    def block_terms(pieces):
        source, target, flow_block, weight_block = pieces
        relative = pose_all[:, source] - pose_all[:, target]
        return edge_terms(relative, inv_depth[target], flow_block, weight_block, across, downward)

    def first_pass(state_sum, pieces):
        grad_part, curv_part, _, _, _ = block_terms(pieces)
        target = pieces[1]
        return ((state_sum[0] + jax.ops.segment_sum(grad_part, target, num_segments=FRAMES), state_sum[1] + jax.ops.segment_sum(curv_part, target, num_segments=FRAMES)), None)
    zeros_map = jnp.zeros((FRAMES, PIXELS), jnp.float32)
    (grad_sum, curv_sum), _ = lax.scan(first_pass, (zeros_map, zeros_map), pieces_all)
    inverse = 1.0 / (DAMP_DEPTH + curv_sum)
    scaled = grad_sum * inverse

    def second_pass(state_sum, pieces):
        _, _, coupling, block, pose_grad = block_terms(pieces)
        source, target = (pieces[0], pieces[1])
        reduced = block - jnp.einsum('aep,bep->eab', coupling * inverse[target][None], coupling, precision=PRECISE)
        reduced_grad = pose_grad - jnp.einsum('aep,ep->ea', coupling, scaled[target], precision=PRECISE)
        flat_block = reduced.reshape(-1, 36)
        out_rows = jnp.concatenate([flat_block, reduced_grad], 1)
        in_rows = jnp.concatenate([flat_block, -reduced_grad], 1)
        return (state_sum + jax.ops.segment_sum(out_rows, source, num_segments=FRAMES) + jax.ops.segment_sum(in_rows, target, num_segments=FRAMES), None)
    block_table, _ = lax.scan(second_pass, jnp.zeros((FRAMES, 42), jnp.float32), pieces_all)
    frame_steps = solve_frames(block_table)

    def third_pass(state_sum, pieces):
        _, _, coupling, _, _ = block_terms(pieces)
        source, target = (pieces[0], pieces[1])
        motion = frame_steps[source] - frame_steps[target]
        correction = jnp.einsum('aep,ea->ep', coupling, motion, precision=PRECISE)
        return (state_sum + jax.ops.segment_sum(correction, target, num_segments=FRAMES), None)
    fix_sum, _ = lax.scan(third_pass, zeros_map, pieces_all)
    depth_next = inv_depth + (grad_sum - fix_sum) * inverse
    return (depth_next, frame_steps.T)
```

```python
import functools

import jax
import jax.numpy as jnp
from jax import lax
from jax.experimental import pallas as pl
from jax.experimental.pallas import tpu as pltpu
from jax.sharding import PartitionSpec as P

IMG_H = 48
IMG_W = 64
DAMP_DEPTH = 0.1
LEVENBERG = 0.1
RIDGE = 0.001
TAIL = 8
LANES = 128
PAIRS = [(i, j) for i in range(6) for j in range(i + 1)]
U_AXES = (0, 1, 2, 3, 5)
V_AXES = (0, 1, 2, 4, 5)
F32 = jnp.float32
BF16 = jnp.bfloat16


def split3(x):
    high = x.astype(BF16)
    rest = x - high.astype(F32)
    mid = rest.astype(BF16)
    low = (rest - mid.astype(F32)).astype(BF16)
    return high, mid, low


def pick(hot, parts, dims=((1,), (0,))):
    hot = hot.astype(BF16)
    total = None
    for part in reversed(parts):
        term = lax.dot_general(hot, part, (dims, ((), ())), preferred_element_type=F32)
        total = term if total is None else total + term
    return total


def lane_tiles(width):
    step = LANES if width % LANES == 0 else width
    return [(start, step) for start in range(0, width, step)]


def as_column(row, count):
    across = lax.broadcasted_iota(jnp.int32, (count, count), 1)
    down = lax.broadcasted_iota(jnp.int32, (count, count), 0)
    return jnp.sum(jnp.where(across == down, row, 0.0), axis=1, keepdims=True)


def source_local(device, count, per_frame, frames_dev, shape, axis):
    edge = lax.broadcasted_iota(jnp.int32, shape, axis)
    frame = jnp.zeros(shape, jnp.int32)
    for k in range(1, frames_dev):
        frame = frame + (edge >= k * per_frame).astype(jnp.int32)
    return frame + device * frames_dev


def as_hot(test):
    return jnp.where(test, 1.0, 0.0).astype(F32)


def pack_kernel(dims, flow, weight, depth, aux, out):
    frames_dev, per_frame, width = dims
    edges = frames_dev * per_frame
    for part, ref in enumerate((flow, weight)):
        for comp in range(2):
            for f in range(frames_dev):
                row = (part * 2 + comp) * edges + f * per_frame
                out[0, row : row + per_frame, :] = ref[comp, f, :, :]
    base = 4 * edges
    out[0, base : base + TAIL, :] = aux[...]
    out[0, base : base + frames_dev, :] = depth[...]


def table_kernel(dims, tails, out):
    frames_dev, per_frame, width = dims
    devices = tails.shape[0]
    for d in range(devices):
        for f in range(frames_dev):
            row = d * frames_dev + f
            out[0, row : row + 1, :] = tails[d, f : f + 1, :]
            out[1, row : row + 1, :] = tails[d, frames_dev + f : frames_dev + f + 1, :]


def first_kernel(dims, slot_row, slot_col, rays, block, own, prev, following, gc_prev, gc_own, gc_next, maps, sums, depth3, pose3, acc):
    frames_dev, per_frame, width, group = dims
    edges = frames_dev * per_frame
    d = pl.program_id(0)

    @pl.when(d == 0)
    def _():
        for b, ref in enumerate((prev, own, following)):
            for k, part in enumerate(split3(ref[0])):
                depth3[k, b * group : (b + 1) * group, :] = part
            for k, part in enumerate(split3(ref[1])):
                pose3[k, b * group : (b + 1) * group, :] = part
        acc[...] = jnp.zeros_like(acc)

    base = 4 * edges
    target_row = block[0, base + 2 * frames_dev : base + 2 * frames_dev + 1, 0:edges]
    target_col = as_column(target_row, edges)
    slots = 3 * group
    hot = as_hot(target_col == slot_row[...])
    hot_t = as_hot(slot_col[...] == target_row)
    local = source_local(d, edges, per_frame, frames_dev, (edges, slots), 0)
    src = as_hot(lax.broadcasted_iota(jnp.int32, (edges, slots), 1) == local + group)
    target_depth = pick(hot, [depth3[k] for k in range(3)])
    relative = pick(src - hot, [pose3[k] for k in range(3)])
    grads, curvs = [], []
    for g in range(0, edges, 8):
        rel = relative[g : g + 8, :]
        w0, w1, w2, m0, m1, m2 = [rel[:, i : i + 1] for i in range(6)]
        partial = {}
        grad_row, curv_row = [], []
        for start, step in lane_tiles(width):
            lanes = slice(start, start + step)
            x = rays[0:1, lanes]
            y = rays[1:2, lanes]
            dep = target_depth[g : g + 8, lanes]
            f0 = block[0, g : g + 8, lanes]
            f1 = block[0, edges + g : edges + g + 8, lanes]
            cu = block[0, 2 * edges + g : 2 * edges + g + 8, lanes]
            cv = block[0, 3 * edges + g : 3 * edges + g + 8, lanes]
            x0 = x + w1 - w2 * y + m0 * dep
            x1 = y + w2 * x - w0 + m1 * dep
            x2 = 1.0 + w0 * y - w1 * x + m2 * dep
            q = 1.0 / x2
            u = x0 * q
            v = x1 * q
            ru = f0 - (u - x)
            rv = f1 - (v - y)
            du = q * (m0 - u * m2)
            dv = q * (m1 - v * m2)
            dq = dep * q
            uq = u * q
            vq = v * q
            ju = {0: -y * uq, 1: q + x * uq, 2: -y * q, 3: dq, 5: -u * dq}
            jv = {0: -q - y * vq, 1: x * vq, 2: x * q, 4: dq, 5: -v * dq}
            cud = cu * du
            cvd = cv * dv
            grad_row.append(cud * ru + cvd * rv)
            curv_row.append(cud * du + cvd * dv)
            for a in range(6):
                term = None
                if a in ju:
                    term = cud * ju[a]
                if a in jv:
                    term = cvd * jv[a] if term is None else term + cvd * jv[a]
                maps[0, a, g : g + 8, lanes] = term
            su = {a: cu * ju[a] for a in ju}
            sv = {a: cv * jv[a] for a in jv}

            def add(key, value):
                partial[key] = value if key not in partial else partial[key] + value

            for k, (a, b) in enumerate(PAIRS):
                if a in ju and b in ju:
                    add(k, su[a] * ju[b])
                if a in jv and b in jv:
                    add(k, sv[a] * jv[b])
            for a in range(6):
                if a in ju:
                    add(21 + a, su[a] * ru)
                if a in jv:
                    add(21 + a, sv[a] * rv)
        grads.append(grad_row)
        curvs.append(curv_row)
        lane = lax.broadcasted_iota(jnp.int32, (8, LANES), 1)
        packed = jnp.zeros((8, LANES), F32)
        for k in sorted(partial):
            packed = jnp.where(lane == k, jnp.sum(partial[k], axis=1, keepdims=True), packed)
        sums[g : g + 8, :] = packed

    for index, rows in enumerate((grads, curvs)):
        for t, (start, step) in enumerate(lane_tiles(width)):
            value = jnp.concatenate([row[t] for row in rows], axis=0)
            acc[index, :, start : start + step] += pick(hot_t, split3(value))

    @pl.when(d == pl.num_programs(0) - 1)
    def _():
        gc_prev[...] = acc[:, 0:group, :]
        gc_own[...] = acc[:, group : 2 * group, :]
        gc_next[...] = acc[:, 2 * group : 3 * group, :]


def second_kernel(dims, slot_row, first, tails, maps, sums, prev, own, following, table, back3, acc):
    frames_dev, per_frame, width, group, frames = dims
    edges = frames_dev * per_frame
    d = pl.program_id(0)

    @pl.when(d == 0)
    def _():
        for b, ref in enumerate((prev, own, following)):
            for i in range(2):
                for k, part in enumerate(split3(ref[i])):
                    back3[i, k, b * group : (b + 1) * group, :] = part
        acc[...] = jnp.zeros_like(acc)

    target_row = tails[0, 2 * frames_dev : 2 * frames_dev + 1, 0:edges]
    target_col = as_column(target_row, edges)
    hot = as_hot(target_col == slot_row[...])
    inverse = pick(hot, [back3[0, k] for k in range(3)])
    scaled = pick(hot, [back3[1, k] for k in range(3)])
    rows = []
    for g in range(0, edges, 8):
        partial = {}
        for start, step in lane_tiles(width):
            lanes = slice(start, start + step)
            inv = inverse[g : g + 8, lanes]
            sca = scaled[g : g + 8, lanes]
            e = [maps[0, a, g : g + 8, lanes] for a in range(6)]
            ei = [value * inv for value in e]

            def add(key, value):
                partial[key] = value if key not in partial else partial[key] + value

            for k, (a, b) in enumerate(PAIRS):
                add(k, ei[a] * e[b])
            for a in range(6):
                add(21 + a, e[a] * sca)
        lane = lax.broadcasted_iota(jnp.int32, (8, LANES), 1)
        packed = jnp.zeros((8, LANES), F32)
        for k in sorted(partial):
            packed = jnp.where(lane == k, jnp.sum(partial[k], axis=1, keepdims=True), packed)
        rows.append(sums[g : g + 8, :] - packed)
    edge_rows = split3(jnp.concatenate(rows, axis=0))
    ids = lax.broadcasted_iota(jnp.int32, (frames, edges), 0)
    local = source_local(d, edges, per_frame, frames_dev, (frames, edges), 1)
    src_t = as_hot(ids == local + first[0])
    tgt_t = as_hot(ids.astype(F32) == target_row)
    plus = pick(src_t + tgt_t, edge_rows)
    minus = pick(src_t - tgt_t, edge_rows)
    lane = lax.broadcasted_iota(jnp.int32, (frames, LANES), 1)
    acc[...] += jnp.where(lane < 21, plus, minus)

    @pl.when(d == pl.num_programs(0) - 1)
    def _():
        table[...] = acc[...].T[0 : table.shape[0], :]


def solve_rows(entry):
    factor = {}
    scale = {}
    for i in range(6):
        for j in range(i + 1):
            element = entry(PAIRS.index((i, j)))
            if i == j:
                element = element * (1.0 + LEVENBERG) + RIDGE
            for k in range(j):
                element = element - factor[i, k] * factor[j, k]
            if i == j:
                factor[i, j] = jnp.sqrt(element)
                scale[i] = 1.0 / factor[i, j]
            else:
                factor[i, j] = element * scale[j]
    forward = []
    for i in range(6):
        element = entry(21 + i)
        for k in range(i):
            element = element - factor[i, k] * forward[k]
        forward.append(element * scale[i])
    result = [None] * 6
    for i in reversed(range(6)):
        element = forward[i]
        for k in range(i + 1, 6):
            element = element - factor[k, i] * result[k]
        result[i] = element * scale[i]
    return result


def third_kernel(dims, slot_col, first, tails, maps, *refs):
    frames_dev, per_frame, width, group, frames, count = dims
    tables = refs[:count]
    z_prev, z_own, z_next, step_out, step3, acc = refs[count:]
    edges = frames_dev * per_frame
    d = pl.program_id(0)

    @pl.when(d == 0)
    def _():
        total = tables[0][...]
        for ref in tables[1:]:
            total = total + ref[...]
        result = solve_rows(lambda k: total[k : k + 1, :])
        stacked = jnp.concatenate(result + [jnp.zeros((2, frames), F32)], axis=0)
        step_out[...] = stacked
        for k, part in enumerate(split3(stacked)):
            step3[k] = part
        acc[...] = jnp.zeros_like(acc)

    target_row = tails[0, 2 * frames_dev : 2 * frames_dev + 1, 0:edges]
    target_col = as_column(target_row, edges)
    hot_t = as_hot(slot_col[...] == target_row)
    ids = lax.broadcasted_iota(jnp.int32, (edges, frames), 1)
    local = source_local(d, edges, per_frame, frames_dev, (edges, frames), 0)
    pair = as_hot(ids == local + first[0]) - as_hot(ids.astype(F32) == target_col)
    motion = pick(pair, [step3[k] for k in range(3)], ((1,), (1,)))
    blocks = []
    for g in range(0, edges, 8):
        move = [motion[g : g + 8, a : a + 1] for a in range(6)]
        row = []
        for start, step in lane_tiles(width):
            lanes = slice(start, start + step)
            value = maps[0, 0, g : g + 8, lanes] * move[0]
            for a in range(1, 6):
                value = value + maps[0, a, g : g + 8, lanes] * move[a]
            row.append(value)
        blocks.append(row)
    for t, (start, step) in enumerate(lane_tiles(width)):
        value = jnp.concatenate([row[t] for row in blocks], axis=0)
        acc[:, start : start + step] += pick(hot_t, split3(value))

    @pl.when(d == pl.num_programs(0) - 1)
    def _():
        z_prev[...] = acc[0:group, :]
        z_own[...] = acc[group : 2 * group, :]
        z_next[...] = acc[2 * group : 3 * group, :]


def shift(values, axis, by):
    count = lax.axis_size(axis)
    return lax.ppermute(values, axis, [(i, (i + by) % count) for i in range(count)])


def chip_partner(values, step):
    count = lax.axis_size("col")
    chips = count // 2
    pairs = []
    for i in range(count):
        chip, core = i // 2, i % 2
        other = chip ^ step if chips & (chips - 1) == 0 else (chip + step) % chips
        pairs.append((i, other * 2 + core))
    return lax.ppermute(values, "col", pairs)


def core_partner(values):
    count = lax.axis_size("col")
    return lax.ppermute(values, "col", [(i, i ^ 1) for i in range(count)])


def whole(shape):
    return pl.BlockSpec(shape, lambda d: (0,) * len(shape))


def params():
    return pltpu.CompilerParams(dimension_semantics=("arbitrary",), vmem_limit_bytes=24 * 1024 * 1024)


def pack_blocks(flow_obs, weight, inv_depth, aux, columns):
    frames_dev, pixels = inv_depth.shape
    per_frame = flow_obs.shape[2]
    edges = frames_dev * per_frame
    width = pixels // columns
    rows = 4 * edges + TAIL
    if width % LANES:
        def cut(values):
            return values.reshape(-1, columns, width).transpose(1, 0, 2)

        tail = jnp.broadcast_to(aux[None, frames_dev:], (columns, TAIL - frames_dev, width))
        return jnp.concatenate([cut(flow_obs), cut(weight), cut(inv_depth), tail], axis=1)
    return pl.pallas_call(
        functools.partial(pack_kernel, (frames_dev, per_frame, width)),
        grid=(columns,),
        in_specs=[
            pl.BlockSpec((2, frames_dev, per_frame, width), lambda j: (0, 0, 0, j)),
            pl.BlockSpec((2, frames_dev, per_frame, width), lambda j: (0, 0, 0, j)),
            pl.BlockSpec((frames_dev, width), lambda j: (0, j)),
            whole((TAIL, width)),
        ],
        out_specs=pl.BlockSpec((1, rows, width), lambda j: (j, 0, 0)),
        out_shape=jax.ShapeDtypeStruct((columns, rows, width), F32),
        compiler_params=params(),
        name="pack",
    )(flow_obs, weight, inv_depth, aux)


def shards(inv_depth, rotation, translation, edge_target, flow_obs, weight):
    frames_dev, pixels = inv_depth.shape
    per_frame = edge_target.shape[1]
    edges = frames_dev * per_frame
    columns = lax.axis_size("col")
    loop_size = lax.axis_size("row")
    group = frames_dev * columns
    frames = group * loop_size
    slots = 3 * group
    width = pixels // columns
    rows = 4 * edges + TAIL
    my_row = lax.axis_index("row")
    my_col = lax.axis_index("col")
    first = (my_row * group).astype(jnp.int32).reshape(1)

    pose = jnp.concatenate([rotation, translation], 0).T
    aux = jnp.concatenate(
        [
            jnp.zeros((frames_dev, width), F32),
            jnp.pad(pose, ((0, 0), (0, width - 6))),
            jnp.pad(edge_target.astype(F32).reshape(1, edges), ((0, 0), (0, width - edges))),
            jnp.zeros((TAIL - 2 * frames_dev - 1, width), F32),
        ],
        0,
    )
    packed = pack_blocks(flow_obs, weight, inv_depth, aux, columns)
    blocks = lax.all_to_all(packed, "col", 0, 0, tiled=True)

    tails_spec = pl.BlockSpec((columns, TAIL, width), lambda d: (0, 4 * edges // TAIL, 0))
    own_table = pl.pallas_call(
        functools.partial(table_kernel, (frames_dev, per_frame, width)),
        grid=(1,),
        in_specs=[tails_spec],
        out_specs=whole((2, group, width)),
        out_shape=jax.ShapeDtypeStruct((2, group, width), F32),
        compiler_params=params(),
        name="gather_table",
    )(blocks)
    prev_table = shift(own_table, "row", 1)
    next_table = shift(own_table, "row", -1)

    slot = jnp.arange(slots, dtype=jnp.int32)
    slot_id = ((my_row - 1 + slot // group + loop_size) % loop_size) * group + slot % group
    slot_row = slot_id.astype(F32).reshape(1, slots)
    slot_col = slot_id.astype(F32).reshape(slots, 1)
    index = my_col * width + jnp.arange(width, dtype=jnp.int32)
    across = (index % IMG_W).astype(F32)
    downward = (index // IMG_W).astype(F32)
    rays = jnp.stack([(across + 0.5) / IMG_W - 0.5, (downward + 0.5 - 0.5 * IMG_H) / IMG_W])

    smem = pl.BlockSpec(memory_space=pltpu.SMEM)
    one_tail = pl.BlockSpec((1, TAIL, width), lambda d: (d, 4 * edges // TAIL, 0))
    maps_spec = pl.BlockSpec((1, 6, edges, width), lambda d: (d, 0, 0, 0))
    sums_spec = pl.BlockSpec((edges, LANES), lambda d: (d, 0))
    pair_shape = jax.ShapeDtypeStruct((2, group, width), F32)
    gc_prev, gc_own, gc_next, maps, sums = pl.pallas_call(
        functools.partial(first_kernel, (frames_dev, per_frame, width, group)),
        grid=(columns,),
        in_specs=[
            whole((1, slots)),
            whole((slots, 1)),
            whole((2, width)),
            pl.BlockSpec((1, rows, width), lambda d: (d, 0, 0)),
        ]
        + [whole((2, group, width))] * 3,
        out_specs=[whole((2, group, width))] * 3 + [maps_spec, sums_spec],
        out_shape=[pair_shape] * 3
        + [
            jax.ShapeDtypeStruct((columns, 6, edges, width), F32),
            jax.ShapeDtypeStruct((columns * edges, LANES), F32),
        ],
        scratch_shapes=[
            pltpu.VMEM((3, slots, width), BF16),
            pltpu.VMEM((3, slots, width), BF16),
            pltpu.VMEM((2, slots, width), F32),
        ],
        compiler_params=params(),
        name="first_pass",
    )(slot_row, slot_col, rays, blocks, own_table, prev_table, next_table)

    sums_gc = gc_own + shift(gc_next, "row", 1) + shift(gc_prev, "row", -1)
    grad_sum = sums_gc[0]
    inverse = 1.0 / (DAMP_DEPTH + sums_gc[1])
    back_own = jnp.stack([inverse, grad_sum * inverse])
    back_prev = shift(back_own, "row", 1)
    back_next = shift(back_own, "row", -1)

    table = pl.pallas_call(
        functools.partial(second_kernel, (frames_dev, per_frame, width, group, frames)),
        grid=(columns,),
        in_specs=[whole((1, slots)), smem, one_tail, maps_spec, sums_spec] + [whole((2, group, width))] * 3,
        out_specs=whole((32, frames)),
        out_shape=jax.ShapeDtypeStruct((32, frames), F32),
        scratch_shapes=[pltpu.VMEM((2, 3, slots, width), BF16), pltpu.VMEM((frames, LANES), F32)],
        compiler_params=params(),
        name="second_pass",
    )(slot_row, first, blocks, maps, sums, back_prev, back_own, back_next)

    arrived = [chip_partner(table, step) for step in range(1, columns // 2)]
    for value in arrived:
        table = table + value
    table = table + core_partner(table)
    tables = [table] + [shift(table, "row", by) for by in range(1, loop_size)]

    z_shape = jax.ShapeDtypeStruct((group, width), F32)
    z_prev, z_own, z_next, step = pl.pallas_call(
        functools.partial(third_kernel, (frames_dev, per_frame, width, group, frames, loop_size)),
        grid=(columns,),
        in_specs=[whole((slots, 1)), smem, one_tail, maps_spec] + [whole((32, frames))] * loop_size,
        out_specs=[whole((group, width))] * 3 + [whole((8, frames))],
        out_shape=[z_shape] * 3 + [jax.ShapeDtypeStruct((8, frames), F32)],
        scratch_shapes=[pltpu.VMEM((3, 8, frames), BF16), pltpu.VMEM((slots, width), F32)],
        compiler_params=params(),
        name="third_pass",
    )(slot_col, first, blocks, maps, *tables)

    fix = z_own + shift(z_next, "row", 1) + shift(z_prev, "row", -1)
    depth_chunk = own_table[0] + (grad_sum - fix) * inverse
    gathered = lax.all_to_all(depth_chunk.reshape(columns, frames_dev, width), "col", 0, 0, tiled=True)
    depth_next = gathered.transpose(1, 0, 2).reshape(frames_dev, pixels)
    first_own = (my_row * columns + my_col) * frames_dev
    pose_step = lax.dynamic_slice(step, (0, first_own), (6, frames_dev))
    return depth_next, pose_step


def solution(mesh):
    return jax.shard_map(
        shards,
        mesh=mesh,
        in_specs=(
            P(("row", "col"), None),
            P(None, ("row", "col")),
            P(None, ("row", "col")),
            P(("row", "col"), None),
            P(None, ("row", "col"), None, None),
            P(None, ("row", "col"), None, None),
        ),
        out_specs=(P(("row", "col"), None), P(None, ("row", "col"))),
        check_vma=False,
    )
```

```python
import functools

import jax
import jax.numpy as jnp
from jax import lax
from jax.experimental import pallas as pl
from jax.experimental.pallas import tpu as pltpu
from jax.sharding import PartitionSpec as P


IMG_H = 48
IMG_W = 64
DAMP_DEPTH = 0.1
LEVENBERG = 0.1
RIDGE = 0.001
TAIL = 8
LANES = 128
U_AXES = (0, 1, 2, 3, 5)
V_AXES = (0, 1, 2, 4, 5)
PAIRS = [(i, j) for i in range(6) for j in range(i + 1)]
F32 = jnp.float32
BF16 = jnp.bfloat16
VMEM = pl.BlockSpec(memory_space=pltpu.VMEM)
SMEM = pl.BlockSpec(memory_space=pltpu.SMEM)


def call(kernel, ins, outs, scratch=(), specs=None, flops=1_000_000):
    shapes = [jax.ShapeDtypeStruct(*out) for out in outs]
    return pl.pallas_call(
        kernel,
        in_specs=specs or [VMEM] * len(ins),
        out_specs=[VMEM] * len(shapes),
        out_shape=shapes,
        scratch_shapes=list(scratch),
        compiler_params=pltpu.CompilerParams(vmem_limit_bytes=28 * 1024 * 1024),
        cost_estimate=pl.CostEstimate(flops=flops, bytes_accessed=0, transcendentals=0),
    )(*ins)


def split3(x):
    high = x.astype(BF16)
    rest = x - high.astype(F32)
    mid = rest.astype(BF16)
    low = (rest - mid.astype(F32)).astype(BF16)
    return high, mid, low


def stack3(x):
    return jnp.concatenate(split3(x), axis=0)


def dot(a, b, dims=((1,), (0,))):
    return lax.dot_general(a, b, (dims, ((), ())), preferred_element_type=F32)


def dot3(hot, x, dims):
    high, mid, low = split3(x)
    return dot(hot, low, dims) + dot(hot, mid, dims) + dot(hot, high, dims)


DOWN = ((0,), (0,))
ACROSS = ((1,), (1,))


def lane_tiles(width):
    step = LANES if width % LANES == 0 else width
    return [slice(start, start + step) for start in range(0, width, step)]


def as_column(row, count):
    across = lax.broadcasted_iota(jnp.int32, (count, count), 1)
    down = lax.broadcasted_iota(jnp.int32, (count, count), 0)
    return jnp.sum(jnp.where(across == down, row, 0.0), axis=1, keepdims=True)


def local_source(device, shape, per_frame, frames_dev):
    edge = lax.broadcasted_iota(jnp.int32, shape, 0)
    frame = jnp.zeros(shape, jnp.int32)
    for k in range(1, frames_dev):
        frame = frame + (edge >= k * per_frame).astype(jnp.int32)
    return frame + device * frames_dev


def as_hot(test):
    return jnp.where(test, 1.0, 0.0).astype(F32)


def near(offset, rows):
    offset = offset % rows
    return offset if offset <= 1 else offset - rows


def sent_blocks(by, rows):
    return [o for o in (-1, 0, 1) if near(o + by, rows) in (-1, 0, 1)]


def reduce_lanes(partial):
    lane = lax.broadcasted_iota(jnp.int32, (8, LANES), 1)
    packed = jnp.zeros((8, LANES), F32)
    for k in sorted(partial):
        packed = jnp.where(lane == k, jnp.sum(partial[k], axis=1, keepdims=True), packed)
    return packed


class Sums(dict):
    def put(self, key, value):
        self[key] = value if key not in self else self[key] + value


def copy_kernel(count, *refs):
    for k in range(count):
        refs[1 + count + k][...] = refs[1 + k][...]


def cut_for_chips(values, chip, chips, axis_of):
    width = values.shape[2] // chips
    ids = jnp.stack([axis_of(chip, s) for s in range(chips)]).astype(jnp.int32)
    if width % LANES:
        return [
            lax.dynamic_slice_in_dim(values, ids[s] * width, width, axis=2) for s in range(chips)
        ]
    shape = values.shape[:2] + (width,)
    return pl.pallas_call(
        functools.partial(copy_kernel, chips),
        grid_spec=pltpu.PrefetchScalarGridSpec(
            num_scalar_prefetch=1,
            grid=(1,),
            in_specs=[
                pl.BlockSpec(shape, lambda i, ids, s=s: (0, 0, ids[s])) for s in range(chips)
            ],
            out_specs=[pl.BlockSpec(shape, lambda i, ids: (0, 0, 0))] * chips,
        ),
        out_shape=[jax.ShapeDtypeStruct(shape, F32)] * chips,
        compiler_params=pltpu.CompilerParams(vmem_limit_bytes=28 * 1024 * 1024),
        name="cut",
    )(ids, *([values] * chips))


def mark_kernel(source, out):
    out[...] = source[0:8, :] + 1.0


def mark(values):
    (out,) = call(mark_kernel, [values], [((8, values.shape[1]), F32)], flops=100)
    return out


def halve_kernel(width, core, *refs):
    refs = refs[1:]
    count = len(refs) - 2
    keep, send = refs[count:]
    mine = pl.multiple_of(core[0] * width, LANES)
    other = pl.multiple_of((1 - core[0]) * width, LANES)
    for s in range(count):
        rows = refs[s].shape[1]
        keep[:, s * rows : (s + 1) * rows, :] = refs[s][:, :, pl.ds(mine, width)]
        send[:, s * rows : (s + 1) * rows, :] = refs[s][:, :, pl.ds(other, width)]


def halve(parts, core, after):
    width = parts[0].shape[2] // 2
    if width % LANES:
        whole = jnp.concatenate(lax.optimization_barrier((*parts, after))[:-1], axis=1)
        return [
            lax.dynamic_slice_in_dim(whole, start * width, width, axis=2) for start in (core, 1 - core)
        ]
    shape = (parts[0].shape[0], len(parts) * parts[0].shape[1], width)
    return call(
        functools.partial(halve_kernel, width),
        [core.astype(jnp.int32).reshape(1), after, *parts],
        [(shape, F32)] * 2,
        specs=[SMEM] + [VMEM] * (len(parts) + 1),
    )


def table_kernel(dims, devices, first, ids, slot_at, tails, tails_other, table, hot, pair, plus, minus):
    frames_dev, per_frame, _, group, frames = dims
    edges = frames_dev * per_frame
    chips = tails.shape[1] // TAIL
    wide = ids.shape[1]
    for h, ref in enumerate((tails, tails_other)):
        for s in range(chips):
            j = h * chips + s
            dev = devices[j]
            for f in range(frames_dev):
                row = dev * frames_dev + f
                table[0, pl.ds(row, 1), :] = ref[0, s * TAIL + f : s * TAIL + f + 1, :]
                at = s * TAIL + frames_dev + f
                table[1, pl.ds(row, 1), :] = ref[0, at : at + 1, :]
            at = s * TAIL + 2 * frames_dev
            column = as_column(ref[0, at : at + 1, 0:edges], edges)
            here = slice(j * edges, (j + 1) * edges)
            target = as_hot(column == ids[...])
            local = local_source(dev, (edges, wide), per_frame, frames_dev)
            hot[here, :] = target.astype(BF16)
            pair[here, :] = (as_hot(slot_at[...] == local + group) - target).astype(BF16)
            frame = lax.broadcasted_iota(jnp.int32, (edges, frames), 1)
            source = as_hot(frame == local_source(dev, (edges, frames), per_frame, frames_dev) + first[0])
            target = as_hot(frame.astype(F32) == column)
            plus[here, :] = (source + target).astype(BF16)
            minus[here, :] = (source - target).astype(BF16)


def geometry(rel, rays, lanes, dep):
    w0, w1, w2, m0, m1, m2 = [rel[:, i : i + 1] for i in range(6)]
    x = rays[0:1, lanes]
    y = rays[1:2, lanes]
    x0 = x + w1 - w2 * y + m0 * dep
    x1 = y + w2 * x - w0 + m1 * dep
    x2 = 1.0 + w0 * y - w1 * x + m2 * dep
    q = 1.0 / x2
    u = x0 * q
    v = x1 * q
    dq = dep * q
    uq = u * q
    vq = v * q
    ju = {0: -y * uq, 1: q + x * uq, 2: -y * q, 3: dq, 5: -u * dq}
    jv = {0: -q - y * vq, 1: x * vq, 2: x * q, 4: dq, 5: -v * dq}
    du = q * (m0 - u * m2)
    dv = q * (m1 - v * m2)
    return u - x, v - y, du, dv, ju, jv


def for_groups(count, body, unroll=2):
    lax.fori_loop(0, count, lambda g, carry: (body(g), carry)[1], 0, unroll=unroll)


def weight_kernel(dims, rays, keep, got, own, prev, following, hot, pair, *refs):
    _, rows, width = dims
    sends = refs[: rows - 1]
    stay, maps, slopes, lean_u, lean_v, sums, depth_e, rel_e, curv = refs[rows - 1 :]
    half = keep.shape[1]
    table = [jnp.concatenate([ref[i] for ref in (prev, own, following)], axis=0) for i in range(2)]
    depth_e[...] = dot(hot[...], stack3(table[0]))
    rel_e[...] = dot(pair[...], stack3(table[1][:, 0 : rel_e.shape[1]]))

    for h, ref in enumerate((keep, got)):

        def body(g, h=h, ref=ref):
            at = pl.ds(pl.multiple_of(g * 8, 8), 8)
            to = pl.ds(pl.multiple_of(h * half + g * 8, 8), 8)
            rel = rel_e[to, :]
            partial = Sums()
            for lanes in lane_tiles(width):
                pu, pv, du, dv, ju, jv = geometry(rel, rays, lanes, depth_e[to, lanes])
                cu = ref[0, at, lanes]
                cv = ref[1, at, lanes]
                cud = cu * du
                cvd = cv * dv
                curv[to, lanes] = cud * du + cvd * dv
                for k, value in enumerate((cud, cvd, pu, pv)):
                    slopes[k, to, lanes] = value
                for a in range(6):
                    terms = [cud * ju[a]] if a in ju else []
                    if a in jv:
                        terms.append(cvd * jv[a])
                    maps[a, to, lanes] = sum(terms[1:], terms[0])
                su = {a: cu * ju[a] for a in ju}
                sv = {a: cv * jv[a] for a in jv}
                for k, (a, c) in enumerate(zip(ju, jv)):
                    lean_u[k, to, lanes] = su[a]
                    lean_v[k, to, lanes] = sv[c]
                for k, (a, b) in enumerate(PAIRS):
                    if a in ju and b in ju:
                        partial.put(k, su[a] * ju[b])
                    if a in jv and b in jv:
                        partial.put(k, sv[a] * jv[b])
            sums[to, :] = reduce_lanes(partial)

        for_groups(half // 8, body)
    scatter(dims, hot, curv[...], sends, stay)


def scatter(dims, hot, values, sends, stay):
    group, rows, _ = dims
    total = dot3(hot[:, 0 : 3 * group], values, DOWN)
    stay[...] = total
    for by, ref in enumerate(sends, 1):
        for k, o in enumerate(sent_blocks(by, rows)):
            ref[k * group : (k + 1) * group, :] = total[(o + 1) * group : (o + 2) * group, :]


def gathered(dims, stay, arrived):
    group, rows, _ = dims
    blocks = [stay[o * group : (o + 1) * group, :] for o in range(3)]
    for by, ref in enumerate(arrived, 1):
        for k, o in enumerate(sent_blocks(by, rows)):
            to = near(o + by, rows) + 1
            blocks[to] = blocks[to] + ref[k * group : (k + 1) * group, :]
    return jnp.concatenate(blocks, axis=0)


def flow_kernel(dims, keep, got, slopes, hot, *refs):
    _, rows, _ = dims
    sends = refs[: rows - 1]
    stay = refs[rows - 1]
    half = keep.shape[1]
    values = []
    for h, ref in enumerate((keep, got)):
        at = slice(h * half, (h + 1) * half)
        ru = ref[0] - slopes[2, at, :]
        rv = ref[1] - slopes[3, at, :]
        values.append(slopes[0, at, :] * ru + slopes[1, at, :] * rv)
    scatter(dims, hot, jnp.concatenate(values, axis=0), sends, stay)


def gradient_kernel(dims, slopes, lean_u, lean_v, flows, flows_got, sums):
    _, _, width = dims
    half = flows.shape[1]
    for h, obs in enumerate((flows, flows_got)):

        def body(g, h=h, obs=obs):
            at = pl.ds(pl.multiple_of(g * 8, 8), 8)
            to = pl.ds(pl.multiple_of(h * half + g * 8, 8), 8)
            partial = Sums()
            for lanes in lane_tiles(width):
                ru = obs[0, at, lanes] - slopes[2, to, lanes]
                rv = obs[1, at, lanes] - slopes[3, to, lanes]
                for k in range(5):
                    partial.put(21 + U_AXES[k], lean_u[k, to, lanes] * ru)
                    partial.put(21 + V_AXES[k], lean_v[k, to, lanes] * rv)
            sums[to, :] = reduce_lanes(partial)

        for_groups(half // 8, body, 4)


def curvature_kernel(dims, maps, sums, hot, plus, *refs):
    _, rows, width = dims
    stay, arrived = refs[0], refs[1:rows]
    inverse, table, inverse_e, edge_rows = refs[rows:]
    inv = 1.0 / (DAMP_DEPTH + gathered(dims, stay, arrived))
    inverse[...] = inv
    inverse_e[...] = dot(hot[...], stack3(inv))

    def body(g):
        to = pl.ds(pl.multiple_of(g * 8, 8), 8)
        partial = Sums()
        for lanes in lane_tiles(width):
            e = [maps[a, to, lanes] for a in range(6)]
            scaled = [value * inverse_e[to, lanes] for value in e]
            for k, (a, b) in enumerate(PAIRS):
                partial.put(k, scaled[a] * e[b])
        edge_rows[to, :] = sums[to, :] - reduce_lanes(partial)

    for_groups(maps.shape[1] // 8, body, 4)
    table[...] = dot3(plus[...], edge_rows[...], DOWN).T[0:32, :]


def schur_kernel(dims, maps, sums, hot, minus, inverse, square, *refs):
    group, rows, width = dims
    stay, arrived = refs[0], refs[1:rows]
    table, keep, scaled_e, edge_rows = refs[rows:]
    grad = gathered(dims, stay, arrived)
    keep[0] = grad[group : 2 * group, :]
    keep[1] = inverse[group : 2 * group, :]
    scaled_e[...] = dot(hot[...], stack3(grad * inverse[...]))

    def body(g):
        to = pl.ds(pl.multiple_of(g * 8, 8), 8)
        partial = Sums()
        for lanes in lane_tiles(width):
            sca = scaled_e[to, lanes]
            for a in range(6):
                partial.put(21 + a, maps[a, to, lanes] * sca)
        edge_rows[to, :] = sums[to, :] - reduce_lanes(partial)

    for_groups(maps.shape[1] // 8, body, 4)
    table[...] = square[...] + dot3(minus[...], edge_rows[...], DOWN).T[0:32, :]


def add_kernel(*refs):
    total = refs[0][...]
    for ref in refs[1:-1]:
        total = total + ref[...]
    refs[-1][...] = total


def solve_rows(entry):
    factor = {}
    scale = {}
    for i in range(6):
        for j in range(i + 1):
            element = entry(PAIRS.index((i, j)))
            if i == j:
                element = element * (1.0 + LEVENBERG) + RIDGE
            for k in range(j):
                element = element - factor[i, k] * factor[j, k]
            if i == j:
                factor[i, j] = jnp.sqrt(element)
                scale[i] = 1.0 / factor[i, j]
            else:
                factor[i, j] = element * scale[j]
    forward = []
    for i in range(6):
        element = entry(21 + i)
        for k in range(i):
            element = element - factor[i, k] * forward[k]
        forward.append(element * scale[i])
    result = [None] * 6
    for i in reversed(range(6)):
        element = forward[i]
        for k in range(i + 1, 6):
            element = element - factor[k, i] * result[k]
        result[i] = element * scale[i]
    return result


def solve_kernel(dims, maps, hot, minus, *refs):
    group, rows, width = dims
    tables = refs[:rows]
    z_prev, z_own, z_next, step_out, motion_e, fix = refs[rows:]
    total = tables[0][...]
    for ref in tables[1:]:
        total = total + ref[...]
    result = solve_rows(lambda k: total[k : k + 1, :])
    steps = jnp.concatenate(result + [jnp.zeros((2, total.shape[1]), F32)], axis=0)
    step_out[...] = steps
    motion_e[...] = dot3(minus[...], steps, ACROSS)

    def body(g):
        to = pl.ds(pl.multiple_of(g * 8, 8), 8)
        motion = motion_e[to, :]
        move = [motion[:, a : a + 1] for a in range(6)]
        for lanes in lane_tiles(width):
            value = maps[0, to, lanes] * move[0]
            for a in range(1, 6):
                value = value + maps[a, to, lanes] * move[a]
            fix[to, lanes] = value

    for_groups(maps.shape[1] // 8, body, 4)
    total = dot3(hot[:, 0 : 3 * group], fix[...], DOWN)
    z_prev[...] = total[0:group, :]
    z_own[...] = total[group : 2 * group, :]
    z_next[...] = total[2 * group : 3 * group, :]


def update_kernel(table, keep, z_own, from_prev, from_next, out):
    out[...] = table[0] + (keep[0] - (z_own[...] + from_prev[...] + from_next[...])) * keep[1]


def sort_kernel(frames_dev, core, table, keep, z_own, from_prev, from_next, stay, send, chunk):
    chunk[...] = table[0] + (keep[0] - (z_own[...] + from_prev[...] + from_next[...])) * keep[1]
    mine = core[0] * frames_dev
    other = (1 - core[0]) * frames_dev
    for chip in range(chunk.shape[0] // (2 * frames_dev)):
        base = chip * 2 * frames_dev
        for f in range(frames_dev):
            row = chip * frames_dev + f
            stay[row : row + 1, :] = chunk[pl.ds(base + mine + f, 1), :]
            send[row : row + 1, :] = chunk[pl.ds(base + other + f, 1), :]


def join_kernel(frames_dev, width, core, ids, stay, got, *outs):
    mine = pl.multiple_of(core[0] * width, LANES)
    other = pl.multiple_of((1 - core[0]) * width, LANES)
    for s, out in enumerate(outs):
        for f in range(frames_dev):
            row = ids[s] * frames_dev + f
            out[f : f + 1, pl.ds(mine, width)] = stay[pl.ds(row, 1), :]
            out[f : f + 1, pl.ds(other, width)] = got[pl.ds(row, 1), :]


def lay_kernel(ids, *refs):
    out = refs[-1]
    for s, ref in enumerate(refs[:-1]):
        width = ref.shape[1]
        out[:, pl.ds(pl.multiple_of(ids[s] * width, LANES), width)] = ref[...]


def shift(values, axis, by):
    count = lax.axis_size(axis)
    return lax.ppermute(values, axis, [(i, (i + by) % count) for i in range(count)])


def other_chip(chip, step, chips):
    return chip ^ step if chips & (chips - 1) == 0 else (step - chip) % chips


def chip_partner(values, step):
    count = lax.axis_size("col")
    chips = count // 2
    pairs = [(i, other_chip(i // 2, step, chips) * 2 + i % 2) for i in range(count)]
    return lax.ppermute(values, "col", pairs)


def core_partner(values):
    count = lax.axis_size("col")
    return lax.ppermute(values, "col", [(i, i ^ 1) for i in range(count)])


def across_chips(parts):
    out = [parts[0]]
    for s, part in enumerate(parts[1:], 1):
        out.append(chip_partner(part, s))
    return out


def shards(inv_depth, rotation, translation, edge_target, flow_obs, weight):
    frames_dev, pixels = inv_depth.shape
    per_frame = edge_target.shape[1]
    edges = frames_dev * per_frame
    columns = lax.axis_size("col")
    chips = columns // 2
    rows = lax.axis_size("row")
    group = frames_dev * columns
    frames = group * rows
    slots = 3 * group
    width = pixels // columns
    total = columns * edges
    my_row = lax.axis_index("row")
    my_col = lax.axis_index("col")
    chip = my_col // 2
    core = my_col % 2
    core_id = core.astype(jnp.int32).reshape(1)
    first = (my_row * group).astype(jnp.int32).reshape(1)
    other = functools.partial(other_chip, chips=chips)
    chip_ids = jnp.stack([other(chip, s) for s in range(chips)]).astype(jnp.int32)
    devices = jnp.concatenate([chip_ids * 2 + core, chip_ids * 2 + (1 - core)]).astype(jnp.int32)

    slot = jnp.arange(slots, dtype=jnp.int32)
    slot_id = ((my_row - 1 + slot // group + rows) % rows) * group + slot % group
    ids3 = jnp.tile(slot_id.astype(F32), 3).reshape(1, 3 * slots)
    slot3 = jnp.tile(slot, 3).reshape(1, 3 * slots)
    index = my_col * width + jnp.arange(width, dtype=jnp.int32)
    across = (index % IMG_W).astype(F32)
    downward = (index // IMG_W).astype(F32)
    rays = jnp.stack([(across + 0.5) / IMG_W - 0.5, (downward + 0.5 - 0.5 * IMG_H) / IMG_W])

    pose = jnp.concatenate([rotation, translation], 0).T
    aux = jnp.concatenate(
        [
            jnp.pad(pose, ((0, 0), (0, width - 6))),
            jnp.pad(edge_target.astype(F32).reshape(1, edges), ((0, 0), (0, width - edges))),
            jnp.zeros((TAIL - 2 * frames_dev - 1, width), F32),
        ],
        0,
    )
    tails = jnp.concatenate([inv_depth, jnp.tile(aux, (1, columns))], 0)

    weight_parts = cut_for_chips(weight.reshape(2, edges, pixels), chip, chips, other)
    tail_parts = cut_for_chips(tails.reshape(1, TAIL, pixels), chip, chips, other)
    flow_parts = cut_for_chips(flow_obs.reshape(2, edges, pixels), chip, chips, other)
    weight_parts = across_chips(weight_parts)
    tail_parts = across_chips(tail_parts)
    flow_parts = across_chips(flow_parts)

    tail_keep, tail_send = halve(tail_parts, core, rays)
    tail_got = core_partner(tail_send)
    own_table, hot, pair, plus, minus = call(
        functools.partial(table_kernel, (frames_dev, per_frame, width, group, frames)),
        [devices, first, ids3, slot3, tail_keep, tail_got],
        [
            ((2, group, width), F32),
            ((total, 3 * slots), BF16),
            ((total, 3 * slots), BF16),
            ((total, frames), BF16),
            ((total, frames), BF16),
        ],
        specs=[SMEM, SMEM, VMEM, VMEM, VMEM, VMEM],
    )
    prev_table = shift(own_table, "row", 1)
    next_table = shift(own_table, "row", -1)

    weight_keep, weight_send = halve(weight_parts, core, mark(own_table[0]))
    weight_got = core_partner(weight_send)
    dims = (group, rows, width)
    send_shapes = [
        ((len(sent_blocks(by, rows)) * group, width), F32) for by in range(1, rows)
    ]
    rel_width = min(width, LANES)
    outs = call(
        functools.partial(weight_kernel, dims),
        [rays, weight_keep, weight_got, own_table, prev_table, next_table, hot, pair],
        send_shapes
        + [
            ((slots, width), F32),
            ((6, total, width), F32),
            ((4, total, width), F32),
            ((5, total, width), F32),
            ((5, total, width), F32),
            ((total, LANES), F32),
        ],
        scratch=[
            pltpu.VMEM((total, width), F32),
            pltpu.VMEM((total, rel_width), F32),
            pltpu.VMEM((total, width), F32),
        ],
    )
    curv_sends = outs[: rows - 1]
    curv_stay, maps, slopes, lean_u, lean_v, sums = outs[rows - 1 :]
    curv_got = []
    for by, part in enumerate(curv_sends, 1):
        curv_got.append(shift(part, "row", -by))
    inverse, square = call(
        functools.partial(curvature_kernel, dims),
        [maps, sums, hot, plus, curv_stay, *curv_got],
        [((slots, width), F32), ((32, frames), F32)],
        scratch=[pltpu.VMEM((total, width), F32), pltpu.VMEM((total, LANES), F32)],
    )

    flow_keep, flow_send = halve(flow_parts, core, mark(curv_stay))
    flow_got = core_partner(flow_send)
    outs = call(
        functools.partial(flow_kernel, dims),
        [flow_keep, flow_got, slopes, hot],
        send_shapes + [((slots, width), F32)],
    )
    grad_sends, grad_stay = outs[: rows - 1], outs[rows - 1]
    grad_got = []
    for by, part in enumerate(grad_sends, 1):
        grad_got.append(shift(part, "row", -by))
    (grad_sums,) = call(
        functools.partial(gradient_kernel, dims),
        [slopes, lean_u, lean_v, flow_keep, flow_got],
        [((total, LANES), F32)],
    )
    table, kept = call(
        functools.partial(schur_kernel, dims),
        [maps, grad_sums, hot, minus, inverse, square, grad_stay, *grad_got],
        [((32, frames), F32), ((2, group, width), F32)],
        scratch=[pltpu.VMEM((total, width), F32), pltpu.VMEM((total, LANES), F32)],
    )

    arrived = [chip_partner(table, step) for step in range(1, chips)]
    (table,) = call(add_kernel, [table, *arrived], [((32, frames), F32)])
    (table,) = call(add_kernel, [table, core_partner(table)], [((32, frames), F32)])
    tables = [table] + [shift(table, "row", by) for by in range(1, rows)]
    z_prev, z_own, z_next, step = call(
        functools.partial(solve_kernel, dims),
        [maps, hot, minus, *tables],
        [((group, width), F32)] * 3 + [((8, frames), F32)],
        scratch=[pltpu.VMEM((total, 8), F32), pltpu.VMEM((total, width), F32)],
    )
    from_prev = shift(z_next, "row", 1)
    from_next = shift(z_prev, "row", -1)
    ends = [own_table, kept, z_own, from_prev, from_next]
    if width % LANES:
        (chunk,) = call(update_kernel, ends, [((group, width), F32)])
        back = lax.all_to_all(chunk.reshape(columns, frames_dev, width), "col", 0, 0, tiled=True)
        depth_next = back.transpose(1, 0, 2).reshape(frames_dev, pixels)
    else:
        stay, send = call(
            functools.partial(sort_kernel, frames_dev),
            [core_id, *ends],
            [((group // 2, width), F32)] * 2,
            scratch=[pltpu.VMEM((group, width), F32)],
            specs=[SMEM] + [VMEM] * 5,
        )
        got = core_partner(send)
        joined = call(
            functools.partial(join_kernel, frames_dev, width),
            [core_id, chip_ids, stay, got],
            [((frames_dev, 2 * width), F32)] * chips,
            specs=[SMEM, SMEM, VMEM, VMEM],
        )
        (depth_next,) = call(
            lay_kernel,
            [chip_ids, *across_chips(joined)],
            [((frames_dev, pixels), F32)],
            specs=[SMEM] + [VMEM] * chips,
        )
    first_own = (my_row * columns + my_col) * frames_dev
    pose_step = lax.dynamic_slice(step, (0, first_own), (6, frames_dev))
    return depth_next, pose_step


def solution(mesh):
    return jax.shard_map(
        shards,
        mesh=mesh,
        in_specs=(
            P(("row", "col"), None),
            P(None, ("row", "col")),
            P(None, ("row", "col")),
            P(("row", "col"), None),
            P(None, ("row", "col"), None, None),
            P(None, ("row", "col"), None, None),
        ),
        out_specs=(P(("row", "col"), None), P(None, ("row", "col"))),
        check_vma=False,
    )
```
